32 devices in a mesh: section: 4 (over y, core), row: 2 (over x), col: 4 (over z).
Axes of the slice: x: 2, y: 2, z: 4, core: 2. Of those that a mesh axis runs over, the one named last changes fastest.
Arguments:
- incoming: bfloat16 [4, 128, 12288], P('section', 'col', 'row'), may hold values from -6 to 6
- loss_grad: bfloat16 [128, 12288], P('col', 'row'), may hold values from -6 to 6
- out_proj_t: bfloat16 [4, 12288, 6144], P('section', 'row', 'col'), may hold values from -0.0546875 to 0.0546875
- query_proj_t: bfloat16 [4, 6144, 12288], P('section', 'col', 'row'), may hold values from -0.078125 to 0.078125
- saved_query: bfloat16 [2, 4, 128, 6144], P(None, 'section', None, 'col'), may hold values from -43 to 43
- saved_key: bfloat16 [2, 4, 128, 6144], P(None, 'section', None, 'col'), may hold values from -4 to 4
- saved_value: bfloat16 [2, 4, 128, 6144], P(None, 'section', None, 'col'), may hold values from -48 to 48
- pattern: int32 [48, 2, 3], replicated, may hold values from 0 to 1, as said below
- plan: int32 [4, 2], replicated, may hold values from 0 to 1, as said below
Outputs:
- handed_first: bfloat16 [4, 128, 12288], P('section', 'col', 'row')
- handed_second: bfloat16 [4, 128, 12288], P('section', 'col', 'row')
The draws below stay inside these ranges and needn't reach their ends.
Inputs may be any that keep to these rules, and one draw needn't show every extreme that they name: pattern[h, i, 0] = i, and every entry of pattern[h, i, :] lies between 0 and i. plan[s, 1] = (plan[s, 0] + 1) % 2.
All inputs are finite; a program needn't handle non-finite values.
Results may differ from the reference program's by a relative error of at most 0.012.
Values may be sent and summed in bfloat16 or wider, within the bound.
No kernel may reach another device: no remote copies, remote signals or barrier semaphores. Data moves between devices by JAX's collectives and lax.ppermute only.
A program may use at most 128 MiB of HBM per device.

```python
import jax
import jax.numpy as jnp
from jax import lax

D = 12288
H = 48
HD = 128
A = 6144
TOKENS = 128
BLOCK = 64
NQB = 2
NATT = 3
SLOTS = 2
SECTIONS = 4


def query_key_pair(key):
    shape = (SLOTS, SECTIONS, TOKENS, A)
    query_key, key_key = jax.random.split(jax.random.fold_in(key, 7), 2)
    key_rows = jnp.clip(jax.random.normal(key_key, shape, jnp.float32), -4.0, 4.0)
    query_rows = jnp.clip(jax.random.normal(query_key, shape, jnp.float32), -4.0, 4.0)
    return (query_rows, key_rows)


def draw_saved_query(key, part):
    return query_key_pair(key)[0].astype(jnp.bfloat16)


def draw_saved_key(key, part):
    return query_key_pair(key)[1].astype(jnp.bfloat16)


def draw_pattern(key, part):
    stride_rows = jax.random.randint(jax.random.fold_in(key, 11), (H, 1, 1), 1, max(NQB, 2))
    block_rows = lax.broadcasted_iota(jnp.int32, (H, NQB, NATT), 1)
    entry_rows = lax.broadcasted_iota(jnp.int32, (H, NQB, NATT), 2)
    candidate = block_rows - entry_rows * stride_rows
    return jnp.where(candidate >= 0, candidate, block_rows).astype(jnp.int32)


def draw_plan(key, part):
    first_slot = jax.random.randint(jax.random.fold_in(key, 13), (SECTIONS, 1), 0, SLOTS)
    second_slot = (first_slot + 1) % SLOTS
    return jnp.concatenate([first_slot, second_slot], axis=1).astype(jnp.int32)


def block_scale(stream_key, dims, cuts, smallest, high):
    loudness, own = 1.0, jax.random.fold_in(stream_key, 6)
    for dim, shards_of in cuts:
        draws = jnp.exp(jax.random.uniform(jax.random.fold_in(own, dim), (shards_of,), jnp.float32, smallest / len(cuts), high / len(cuts)))
        loudness = loudness * jnp.repeat(draws, dims[dim] // shards_of).reshape([-1 if axis == dim else 1 for axis in range(len(dims))])
    return loudness


def normal_values(stream_key, extent, width, most, pieces=(), held_as=jnp.bfloat16):
    level = block_scale(stream_key, extent, pieces, -0.22, 0.18) if pieces else 1.0
    values = jax.random.normal(stream_key, extent, jnp.float32) * width * level
    return jnp.minimum(jnp.maximum(values, -most), most).astype(held_as)


def setup_inputs(seed: int = 0) -> dict:
    streams_of = jax.random.split(jax.random.key(seed), 10)
    return {
        "incoming": normal_values(streams_of[0], (SECTIONS, TOKENS, D), 1.0, 6.0, ((0, 4), (1, 4), (2, 2))),
        "loss_grad": normal_values(streams_of[1], (TOKENS, D), 1.0, 6.0, ((0, 4), (1, 2))),
        "out_proj_t": normal_values(streams_of[2], (SECTIONS, D, A), D ** -0.5, 0.0546875, ((0, 4), (1, 2), (2, 4))),
        "query_proj_t": normal_values(streams_of[3], (SECTIONS, A, D), A ** -0.5, 0.078125, ((0, 4), (1, 4), (2, 2))),
        "saved_query": draw_saved_query(jax.random.fold_in(streams_of[9], 71), 0),
        "saved_key": draw_saved_key(jax.random.fold_in(streams_of[9], 71), 0),
        "saved_value": normal_values(streams_of[6], (SLOTS, SECTIONS, TOKENS, A), 8.0, 48.0, ((1, 4), (3, 4))),
        "pattern": draw_pattern(jax.random.fold_in(streams_of[9], 71), 0),
        "plan": draw_plan(jax.random.fold_in(streams_of[9], 71), 0),
    }


def token_mask(pattern_part, tokens):
    blocks = tokens // BLOCK
    member = jnp.any(pattern_part[:, :, :, None] == jnp.arange(blocks, dtype=jnp.int32)[None, None, None, :], axis=2)
    member = jnp.repeat(jnp.repeat(member, BLOCK, axis=1), BLOCK, axis=2)
    positions = jnp.arange(tokens, dtype=jnp.int32)
    return member & (positions[:, None] >= positions[None, :])[None]


def attend_rows(upstream, query_rows, key_rows, value_rows, allowed):
    row_count = query_rows.shape[0]
    head_count = query_rows.shape[1] // HD
    inverse_root = HD ** -0.5
    q_heads = query_rows.astype(jnp.float32).reshape(row_count, head_count, HD)
    k_heads = key_rows.astype(jnp.float32).reshape(key_rows.shape[0], head_count, HD)
    v_heads = value_rows.astype(jnp.float32).reshape(value_rows.shape[0], head_count, HD)
    up_heads = lax.optimization_barrier(upstream).astype(jnp.float32).reshape(row_count, head_count, HD)
    scores = jnp.einsum('thd,uhd->htu', q_heads, k_heads) * inverse_root
    masked = jnp.where(allowed, scores, -jnp.inf)
    row_peak = jnp.max(masked, axis=-1, keepdims=True)
    exp_terms = jnp.where(allowed, jnp.exp(masked - row_peak), 0.0)
    row_total = jnp.sum(exp_terms, axis=-1, keepdims=True)
    prob_rows = exp_terms / row_total
    prob_grad = jnp.einsum('thd,uhd->htu', up_heads, v_heads)
    row_delta = jnp.sum(prob_rows * prob_grad, axis=-1, keepdims=True)
    dscore = (prob_rows * (prob_grad - row_delta)).astype(jnp.bfloat16)
    dscore = lax.optimization_barrier(dscore).astype(jnp.float32)
    dquery = jnp.einsum('htu,uhd->thd', dscore, k_heads) * inverse_root
    return dquery.reshape(row_count, head_count * HD).astype(jnp.bfloat16)


def reference(incoming, loss_grad, out_proj_t, query_proj_t, saved_query, saved_key, saved_value, pattern, plan):
    allowed = token_mask(pattern, TOKENS)

    def update(section_index, gradient, slot_index):
        upstream = jnp.dot(gradient, out_proj_t[section_index], preferred_element_type=jnp.float32).astype(jnp.bfloat16)
        dquery = attend_rows(upstream, saved_query[slot_index, section_index], saved_key[slot_index, section_index], saved_value[slot_index, section_index], allowed)
        mixed_back = jnp.dot(dquery, query_proj_t[section_index], preferred_element_type=jnp.float32)
        return (gradient.astype(jnp.float32) + mixed_back).astype(jnp.bfloat16)

    first_list = [update(section_index, incoming[section_index], plan[section_index, 0]) for section_index in range(SECTIONS)]
    handed_first = jnp.stack(first_list)
    handed = jnp.concatenate([handed_first[1:], loss_grad[None]], axis=0)
    second_list = [update(section_index, handed[section_index], plan[section_index, 1]) for section_index in range(SECTIONS)]
    handed_second = jnp.stack(second_list)
    return (handed_first, handed_second)
```

```python
import functools

import jax
import jax.numpy as jnp
from jax import lax
from jax.experimental import pallas as pl
from jax.experimental.pallas import tpu as pltpu
from jax.sharding import PartitionSpec as P

HD = 128
BLOCK = 64
INVERSE_ROOT = HD ** (-0.5)
F32 = jnp.float32
BF16 = jnp.bfloat16
FIXED = 3
GRANT = 6 << 20
KEPT = 5

HBM = pl.BlockSpec(memory_space=pltpu.HBM)
VMEM = pl.BlockSpec(memory_space=pltpu.VMEM)
SMEM = pl.BlockSpec(memory_space=pltpu.SMEM)


def chunk_of(size, most):
    return max(c for c in range(HD, most + 1, HD) if size % c == 0)


def ring_order(count):
    return list(range(0, count, 2)) + list(range(1, count, 2))[::-1]


def params(limit):
    return pltpu.CompilerParams(vmem_limit_bytes=limit)


def prepare_kernel(heads, copies, pattern_at, facts, wo, wq, sq, sk, sv, wo_v, wq_v, prob, k_sel, v_sel, q_sel, sem):
    turns, tokens, width = q_sel.shape
    pending = []

    def start(source, target):
        copy = pltpu.make_async_copy(source, target, sem.at[len(pending)])
        copy.start()
        pending.append(copy)

    for turn in range(turns):
        for saved, picked in ((sq, q_sel), (sk, k_sel), (sv, v_sel)):
            start(saved.at[facts[1 + turn]], picked.at[turn])
    early = len(pending)
    for weight, held in ((wo, wo_v), (wq, wq_v)):
        rows = weight.shape[0] // copies
        for i in range(copies):
            start(weight.at[pl.ds(i * rows, rows)], held.at[pl.ds(i * rows, rows)])
    for copy in pending[:early]:
        copy.wait()

    blocks = tokens // BLOCK
    listed = (facts.shape[0] - pattern_at) // (heads * blocks)
    row_at = lax.broadcasted_iota(jnp.int32, (tokens, tokens), 0)
    col_at = lax.broadcasted_iota(jnp.int32, (tokens, tokens), 1)

    def one_head(head, carry):
        lanes = pl.ds(pl.multiple_of(head * HD, HD), HD)
        member = jnp.zeros((tokens, tokens), jnp.int32)
        for i in range(blocks):
            for j in range(blocks):
                flag = jnp.int32(0)
                for e in range(listed):
                    entry = facts[pattern_at + (head * blocks + i) * listed + e]
                    flag = jnp.where(entry == j, jnp.int32(1), flag)
                inside = (row_at // BLOCK == i) & (col_at // BLOCK == j)
                member = jnp.where(inside, flag, member)
        allowed = (member > 0) & (col_at <= row_at)
        for turn in range(turns):
            score = (
                lax.dot_general(
                    q_sel[turn, :, lanes],
                    k_sel[turn, :, lanes],
                    (((1,), (1,)), ((), ())),
                    preferred_element_type=F32,
                )
                * INVERSE_ROOT
            )
            masked = jnp.where(allowed, score, -jnp.inf)
            peak = jnp.max(masked, axis=-1, keepdims=True)
            terms = jnp.where(allowed, jnp.exp(masked - peak), 0.0)
            prob[turn, head] = terms / jnp.sum(terms, axis=-1, keepdims=True)
        return carry

    lax.fori_loop(0, heads, one_head, 0)
    for copy in pending[early:]:
        copy.wait()


def prepare(turns, pattern_at, facts, wo, wq, sq, sk, sv):
    tokens, width = sq.shape[1:]
    heads = width // HD
    copies = 8
    return pl.pallas_call(
        functools.partial(prepare_kernel, heads, copies, pattern_at),
        in_specs=[SMEM] + [HBM] * 5,
        out_specs=[VMEM] * 5,
        out_shape=[
            pltpu.VMEM(wo.shape, BF16),
            pltpu.VMEM(wq.shape, BF16),
            pltpu.VMEM((turns, heads, tokens, tokens), F32),
            pltpu.VMEM((turns, tokens, width), BF16),
            pltpu.VMEM((turns, tokens, width), BF16),
        ],
        scratch_shapes=[
            pltpu.VMEM((turns, tokens, width), BF16),
            pltpu.SemaphoreType.DMA((3 * turns + 2 * copies,)),
        ],
        compiler_params=params(GRANT),
        name="prepare",
    )(facts, *(pltpu.with_memory_space_constraint(x, pltpu.HBM) for x in (wo, wq, sq, sk, sv)))


def entry_kernel(count, *refs):
    parts, weight, out = refs[:count], refs[count + 1], refs[count + 1 + KEPT]
    width = weight.shape[1]
    step_width = chunk_of(width, 512)
    if count == 1:
        source = parts[0]
    else:
        source = refs[count + 2 + KEPT]
        rows = parts[0].shape[0]
        for i, part in enumerate(parts):
            source[i * rows : (i + 1) * rows] = part[...]

    def step(i, carry):
        lanes = pl.ds(pl.multiple_of(i * step_width, step_width), step_width)
        out[:, lanes] = jnp.dot(source[...], weight[:, lanes], preferred_element_type=F32).astype(BF16)
        return carry

    lax.fori_loop(0, width // step_width, step, 0)


def entry(parts, facts, kept):
    weight = kept[0]
    rows = parts[0].shape[0] * len(parts)
    scratch = [pltpu.VMEM((rows, weight.shape[0]), BF16)] if len(parts) > 1 else []
    return pl.pallas_call(
        functools.partial(entry_kernel, len(parts)),
        in_specs=[VMEM] * len(parts) + [SMEM] + [VMEM] * KEPT,
        out_specs=VMEM,
        out_shape=pltpu.VMEM((rows, weight.shape[1]), BF16),
        scratch_shapes=scratch,
        compiler_params=params(GRANT),
        name="entry",
    )(*parts, facts, *kept)


def exit_kernel(turn, steps, mine, theirs, facts, _, weight, prob, keys, values, *refs):
    outs, dquery = refs[: len(steps)], refs[len(steps)]
    heads = mine.shape[1] // HD
    rows = mine.shape[0] // len(steps)
    parts = []
    for s, step_at in enumerate(steps):
        here = slice(s * rows, (s + 1) * rows)
        first = pl.multiple_of(facts[FIXED + step_at] * rows, rows)
        for head in range(heads):
            lanes = slice(head * HD, (head + 1) * HD)
            upstream = (mine[here, lanes].astype(F32) + theirs[here, lanes].astype(F32)).astype(BF16)
            prob_grad = lax.dot_general(
                upstream, values[turn, :, lanes], (((1,), (1,)), ((), ())), preferred_element_type=F32
            )
            parts.append((here, lanes, head, first, prob_grad))
    scored = []
    for here, lanes, head, first, prob_grad in parts:
        weights = prob[turn, head, pl.ds(first, rows), :]
        delta = jnp.sum(weights * prob_grad, axis=-1, keepdims=True)
        scored.append((here, lanes, (weights * (prob_grad - delta)).astype(BF16)))
    backs = [
        (here, lanes, jnp.dot(dscore, keys[turn, :, lanes], preferred_element_type=F32))
        for here, lanes, dscore in scored
    ]
    for here, lanes, back in backs:
        dquery[here, lanes] = (back * INVERSE_ROOT).astype(BF16)
    width = weight.shape[1]
    step_width = chunk_of(width, 1024)

    def step(i, carry):
        lanes = pl.ds(pl.multiple_of(i * step_width, step_width), step_width)
        mixed = jnp.dot(dquery[...], weight[:, lanes], preferred_element_type=F32).astype(BF16)
        for s, out in enumerate(outs):
            out[:, lanes] = mixed[s * rows : (s + 1) * rows]
        return carry

    lax.fori_loop(0, width // step_width, step, 0)


def leave(turn, steps, mine, theirs, facts, kept):
    weight = kept[1]
    rows = mine.shape[0] // len(steps)
    return pl.pallas_call(
        functools.partial(exit_kernel, turn, steps),
        in_specs=[VMEM] * 2 + [SMEM] + [VMEM] * KEPT,
        out_specs=[VMEM] * len(steps),
        out_shape=[pltpu.VMEM((rows, weight.shape[1]), BF16)] * len(steps),
        scratch_shapes=[pltpu.VMEM(mine.shape, BF16)],
        compiler_params=params(GRANT),
        name="leave",
    )(mine, theirs, facts, *kept)


def add_kernel(total, part, *refs):
    out = refs[KEPT + 1]
    out[...] = (total[...].astype(F32) + part[...].astype(F32)).astype(BF16)


def add(total, part, facts, kept):
    return pl.pallas_call(
        add_kernel,
        in_specs=[VMEM] * 2 + [SMEM] + [VMEM] * KEPT,
        out_specs=VMEM,
        out_shape=pltpu.VMEM(part.shape, BF16),
        compiler_params=params(GRANT),
        name="add",
    )(total, part, facts, *kept)


def finish_kernel(own, total, part, loss, facts, *refs):
    handed, payload = refs[KEPT:]
    handed[...] = (own[...].astype(F32) + (total[...].astype(F32) + part[...].astype(F32))).astype(BF16)

    @pl.when(facts[0] == 0)
    def _():
        payload[...] = loss[...]

    @pl.when(facts[0] != 0)
    def _():
        payload[...] = handed[...]


def finish(own, total, part, loss, facts, kept):
    return pl.pallas_call(
        finish_kernel,
        in_specs=[VMEM] * 4 + [SMEM] + [VMEM] * KEPT,
        out_specs=[VMEM] * 2,
        out_shape=[jax.ShapeDtypeStruct(own.shape, BF16), pltpu.VMEM(own.shape, BF16)],
        compiler_params=params(GRANT),
        name="finish",
    )(own, total, part, loss, facts, *kept)


def last_kernel(own, total, part, *refs):
    handed = refs[KEPT + 1]
    handed[...] = (own[...].astype(F32) + (total[...].astype(F32) + part[...].astype(F32))).astype(BF16)


def last(own, total, part, facts, kept):
    return pl.pallas_call(
        last_kernel,
        in_specs=[VMEM] * 3 + [SMEM] + [VMEM] * KEPT,
        out_specs=VMEM,
        out_shape=jax.ShapeDtypeStruct(own.shape, BF16),
        compiler_params=params(GRANT),
        name="last",
    )(own, total, part, facts, *kept)


def body(sizes, incoming, loss_grad, out_proj_t, query_proj_t, saved_query, saved_key, saved_value, pattern, plan):
    sections, rows, cols = sizes
    section_at = lax.axis_index("section")
    col_at = lax.axis_index("col")
    order = ring_order(cols)
    after = {order[i]: order[(i + 1) % cols] for i in range(cols)}
    ring = [(c, after[c]) for c in range(cols)]
    before_section = [(s, (s - 1) % sections) for s in range(sections)]
    joint = [
        (s * cols + c, before * cols + after[c]) for s, before in before_section for c in range(cols)
    ]
    place_table = [[order[(order.index(c) - k) % cols] for k in range(cols)] for c in range(cols)]
    place = lax.dynamic_index_in_dim(jnp.array(place_table, jnp.int32), col_at, 0, keepdims=False)
    slots = lax.dynamic_index_in_dim(plan, section_at, 0, keepdims=False)
    heads = out_proj_t.shape[2] // HD
    local_pattern = lax.dynamic_slice_in_dim(pattern, col_at * heads, heads, 0).reshape(-1)
    facts = jnp.concatenate([section_at[None], slots, place, local_pattern])
    turns = plan.shape[1]

    kept = prepare(
        turns, FIXED + cols, facts, out_proj_t[0], query_proj_t[0], saved_query[:, 0], saved_key[:, 0], saved_value[:, 0]
    )

    def from_other_rows(partial):
        moving, total = partial, None
        for _ in range(rows - 1):
            moving = lax.ppermute(moving, "row", [(r, (r + 1) % rows) for r in range(rows)])
            total = moving if total is None else total + moving
        return jnp.zeros_like(partial) if total is None else total

    def turn_of(own, first, turn):
        def contribution(steps, parts):
            partial = entry(parts, facts, kept)
            return leave(turn, steps, partial, from_other_rows(partial), facts, kept)

        moving = first
        later = []
        for k in range(2, cols):
            moving = lax.ppermute(moving, "col", ring)
            later.append((k, moving))
        own_part, total = contribution((0, 1), (own, first))
        total = lax.ppermute(total, "col", ring)
        for k, moved in later:
            (part,) = contribution((k,), (moved,))
            total = lax.ppermute(add(total, part, facts, kept), "col", ring)
        return total, own_part

    own = incoming[0]
    total, part = turn_of(own, lax.ppermute(own, "col", ring), 0)
    handed_first, payload = finish(own, total, part, loss_grad, facts, kept)
    first = lax.ppermute(payload, ("section", "col"), joint)
    second = lax.ppermute(payload, "section", before_section)
    handed_second = last(second, *turn_of(second, first, 1), facts, kept)
    return (handed_first[None], handed_second[None])


def solution(mesh):
    sizes = tuple(mesh.shape[axis] for axis in ("section", "row", "col"))
    return jax.shard_map(
        functools.partial(body, sizes),
        mesh=mesh,
        in_specs=(
            P("section", "col", "row"),
            P("col", "row"),
            P("section", "row", "col"),
            P("section", "col", "row"),
            P(None, "section", None, "col"),
            P(None, "section", None, "col"),
            P(None, "section", None, "col"),
            P(),
            P(),
        ),
        out_specs=(P("section", "col", "row"), P("section", "col", "row")),
        check_vma=False,
    )
```
